32 devices in a mesh: rve: 4 (over y, x), slab: 8 (over z, core).
Axes of the slice: x: 2, y: 2, z: 4, core: 2. Of those that a mesh axis runs over, the one named last changes fastest.
Arguments:
- plastic_strain: float32 [6, 4, 96, 9216], P(None, 'rve', 'slab'), may hold values from -2 to 2
- hardening_var: float32 [4, 96, 9216], P('rve', 'slab'), may hold values from 0 to 1
- strain_start: float32 [6, 4, 96, 9216], P(None, 'rve', 'slab'), may hold values from -6 to 6
- strain_step: float32 [6, 4, 96, 9216], P(None, 'rve', 'slab'), may hold values from -4 to 4
- shear_mod: float32 [4, 96, 9216], P('rve', 'slab'), may hold values from 0.5 to 2
- bulk_mod: float32 [4, 96, 9216], P('rve', 'slab'), may hold values from 1 to 4
- yield_stress: float32 [4, 96, 9216], P('rve', 'slab'), may hold values from 0.5 to 4
- substeps: int32 [4, 384], replicated, may hold values from 1 to 8, as said below
- pull_group: int32 [4, 16], replicated, may hold values from 0 to 3, as said below
- pull_block: int32 [4, 16], replicated, may hold values from 0 to 383, as said below
- owner: int32 [4], replicated, may hold values from 0 to 3
Outputs:
- correction: float32 [3, 4, 96, 9216], P(None, 'rve', 'slab')
- inbox: float32 [7, 4, 16, 2304], P(None, 'rve', 'slab')
- element_sums: float32 [4, 42], P('rve')
The draws below stay inside these ranges and needn't reach their ends.
Inputs may be any that keep to these rules, and one draw needn't show every extreme that they name: `substeps`: every RVE has a block with exactly its largest count, and some RVE reaches 8. `pull_group`: for each group g and each slab s, the 2 slots k with k // 2 = s name distinct source groups. `pull_block`: slot k names a block of z-slab k // 2: an id from (k // 2) * 4 * 12 to (k // 2 + 1) * 4 * 12 - 1.
All inputs are finite; a program needn't handle non-finite values.
Results may differ from the reference program's by a relative error of at most 0.0003.
Values sent between devices are 32-bit elements; how exact they have to be, the bound alone decides.
A program may use at most 192 MiB of HBM per device.

```python
import math
import jax
import jax.numpy as jnp
from jax import lax

NVX = 96
NZ = 96
ITERS = 5
SUBMAX = 8
SZ = 12
PLANE = 9216
BLK = 2304
NBLK = 384
RVES = 4
IN_DEV = 2
INBOX = 16


def pull_plan(key):
    slab_total = INBOX // IN_DEV
    key_list = jax.random.split(jax.random.fold_in(key, 11), RVES * slab_total)

    def choose(single):
        return jax.random.permutation(single, RVES)[:IN_DEV]
    sources = jax.vmap(choose)(key_list).reshape(RVES, INBOX)
    offsets = jax.random.randint(jax.random.fold_in(key, 12), (RVES, INBOX), 0, 4 * SZ)
    slots = jnp.arange(INBOX)
    blocks = (slots // IN_DEV)[None, :] * (4 * SZ) + offsets
    return (sources.astype(jnp.int32), blocks.astype(jnp.int32))


def draw_pull_group(key, part):
    return pull_plan(key)[0]


def draw_pull_block(key, part):
    return pull_plan(key)[1]


def draw_substeps(key, part):
    level = jax.random.randint(jax.random.fold_in(key, 21), (RVES,), 1, SUBMAX + 1)
    forced = jax.random.randint(jax.random.fold_in(key, 22), (), 0, RVES)
    level = jnp.where(jnp.arange(RVES) == forced, SUBMAX, level)
    raw = jax.random.randint(jax.random.fold_in(key, 23), (RVES, NBLK), 0, 1000000) % level[:, None] + 1
    special = jax.random.randint(jax.random.fold_in(key, 24), (RVES,), 0, NBLK)
    costs = jnp.where(jnp.arange(NBLK)[None, :] == special[:, None], level[:, None], raw)
    return costs.astype(jnp.int32)


def with_ends(values, rng, low, largest):
    extent = values.shape
    index_at = [jax.random.randint(jax.random.fold_in(rng, axis), (), 0, extent[axis]) for axis in range(len(extent))]
    values = values.at[tuple(index_at)].set(low)
    longest = extent.index(max(extent))
    index_at[longest] = (index_at[longest] + 1) % extent[longest]
    return values.at[tuple(index_at)].set(largest)


def block_levels(stream_key, extent, cuts, low, high):
    loudness = 1.0
    for position, shards_of in cuts:
        draws = jax.random.uniform(jax.random.fold_in(jax.random.fold_in(stream_key, 6), position), (shards_of,), jnp.float32, low / len(cuts), high / len(cuts))
        loudness = loudness * jnp.repeat(jnp.exp(draws), extent[position] // shards_of).reshape((-1,) + (1,) * (len(extent) - 1 - position))
    return loudness


def bell_draw(key, shape, deviation, most, shards=(), kind=jnp.bfloat16):
    result = deviation * jax.random.normal(key, shape, jnp.float32)
    if shards:
        result = result * block_levels(key, shape, shards, -0.22, 0.18)
    return jnp.clip(result, -most, most).astype(kind)


def setup_inputs(seed: int = 0) -> dict:
    splits = jax.random.split(jax.random.key(seed), 12)
    plastic_strain = bell_draw(splits[0], (6, RVES, NZ, PLANE), 0.3, 2.0, ((1, 4), (2, 8)), jnp.float32)
    hardening_var = jnp.clip(1.0 * jax.random.uniform(splits[1], (RVES, NZ, PLANE), jnp.float32) ** block_levels(splits[1], (RVES, NZ, PLANE), ((0, 4), (1, 8)), -0.2, 0.2), 0.0, 1.0)
    strain_start = bell_draw(splits[2], (6, RVES, NZ, PLANE), 1.0, 6.0, ((1, 4), (2, 8)), jnp.float32)
    strain_step = bell_draw(splits[3], (6, RVES, NZ, PLANE), 0.5, 4.0, ((1, 4), (2, 8)), jnp.float32)
    shear_mod = jnp.clip(jnp.exp(math.log(2.0) - 1.3862944 * jax.random.uniform(splits[4], (RVES, NZ, PLANE), jnp.float32) ** block_levels(splits[4], (RVES, NZ, PLANE), ((0, 4), (1, 8)), -0.2, 0.2)), 0.5, 2.0)
    bulk_mod = jnp.clip(jnp.exp(math.log(4.0) - 1.3862944 * jax.random.uniform(splits[5], (RVES, NZ, PLANE), jnp.float32) ** block_levels(splits[5], (RVES, NZ, PLANE), ((0, 4), (1, 8)), -0.2, 0.2)), 1.0, 4.0)
    yield_stress = jnp.clip(jnp.exp(math.log(4.0) - 2.0794415 * jax.random.uniform(splits[6], (RVES, NZ, PLANE), jnp.float32) ** block_levels(splits[6], (RVES, NZ, PLANE), ((0, 4), (1, 8)), -0.2, 0.2)), 0.5, 4.0)
    substeps = draw_substeps(jax.random.fold_in(splits[11], 71), 0)
    pull_group = draw_pull_group(jax.random.fold_in(splits[11], 71), 0)
    pull_block = draw_pull_block(jax.random.fold_in(splits[11], 71), 0)
    owner = with_ends(jax.random.randint(splits[10], (RVES,), 0, RVES), jax.random.fold_in(splits[10], 1), 0, RVES - 1).astype(jnp.int32)
    return {"plastic_strain": plastic_strain, "hardening_var": hardening_var, "strain_start": strain_start, "strain_step": strain_step, "shear_mod": shear_mod, "bulk_mod": bulk_mod, "yield_stress": yield_stress, "substeps": substeps, "pull_group": pull_group, "pull_block": pull_block, "owner": owner}


hard_ratio = 0.3
mass_weight = 0.05
root_two_thirds = math.sqrt(2.0 / 3.0)
half_root = 1.0 / math.sqrt(2.0)

def stencil_offsets():
    listing = []
    for depth_step in (-1, 0, 1):
        for row_step in (-1, 0, 1):
            for column_step in (-1, 0, 1):
                reach = abs(depth_step) + abs(row_step) + abs(column_step)
                if reach > 0:
                    listing.append((depth_step, row_step, column_step, (1.0, 0.5, 0.25)[reach - 1]))
    return listing

def plane_shift(values, row_step, column_step):
    if row_step != 0:
        values = jnp.roll(values, -row_step * NVX, axis=-1)
    if column_step != 0:
        column = jnp.arange(PLANE) % NVX
        plain = jnp.roll(values, -column_step, axis=-1)
        wrapped = jnp.roll(values, column_step * NVX - column_step, axis=-1)
        border = NVX - 1 if column_step > 0 else 0
        values = jnp.where(column == border, wrapped, plain)
    return values

def trace_vector(ndim):
    return jnp.array([1.0, 1.0, 1.0, 0.0, 0.0, 0.0], jnp.float32).reshape((6,) + (1,) * (ndim - 1))

def deviator_of(strain, plastic):
    elastic = strain - plastic
    volume = elastic[0] + elastic[1] + elastic[2]
    return (elastic - volume / 3.0 * trace_vector(strain.ndim), volume)

def return_map(plastic, hardening, strain_begin, strain_delta, shear_field, bulk_field, yield_field, count, turns):
    harden = hard_ratio * shear_field

    def substep(turn, carry):
        plastic_now, hardening_now, increment, direction, floored = carry
        turn_float = jnp.asarray(turn).astype(jnp.float32)
        strain = strain_begin + (turn_float + 1.0) / count * strain_delta
        deviator, volume = deviator_of(strain, plastic_now)
        trial = 2.0 * shear_field * deviator
        magnitude = jnp.sqrt(lax.optimization_barrier(jnp.sum(trial * trial, axis=0)))
        excess = magnitude - root_two_thirds * (yield_field + harden * hardening_now)
        active = turn_float < count
        new_increment = jnp.maximum(excess, 0.0) / (2.0 * shear_field + 2.0 / 3.0 * harden)
        new_floored = jnp.maximum(magnitude, root_two_thirds * yield_field)
        new_direction = trial / new_floored
        new_increment = jnp.where(active, new_increment, 0.0)
        plastic_now = plastic_now + new_increment * new_direction
        hardening_now = hardening_now + root_two_thirds * new_increment
        increment = jnp.where(active, new_increment, increment)
        direction = jnp.where(active, new_direction, direction)
        floored = jnp.where(active, new_floored, floored)
        return (plastic_now, hardening_now, increment, direction, floored)
    start = (plastic, hardening, jnp.zeros_like(hardening), jnp.zeros_like(plastic), jnp.ones_like(hardening))
    plastic_new, hardening_new, increment, direction, floored = lax.fori_loop(0, turns, substep, start)
    deviator, volume = deviator_of(strain_begin + strain_delta, plastic_new)
    stress = bulk_field * volume * trace_vector(plastic.ndim) + 2.0 * shear_field * deviator
    theta = 1.0 - 2.0 * shear_field * increment / floored
    coefficient = shear_field * theta
    weight = shear_field * (theta - 1.0)
    return (stress, coefficient, plastic_new, hardening_new, weight, direction)

def rhs_from(stress, depth_diff):
    row_diff = 0.5 * (plane_shift(stress, 1, 0) - plane_shift(stress, -1, 0))
    column_diff = 0.5 * (plane_shift(stress, 0, 1) - plane_shift(stress, 0, -1))
    return jnp.stack([column_diff[0] + half_root * (row_diff[5] + depth_diff[4]), half_root * (column_diff[5] + depth_diff[3]) + row_diff[1], half_root * (column_diff[4] + row_diff[3]) + depth_diff[2]])

def apply_operator(field, coefficient):
    total = mass_weight * coefficient * field
    for depth_step, row_step, column_step, weight in stencil_offsets():
        other = plane_shift(jnp.roll(field, -depth_step, axis=-2), row_step, column_step)
        other_coef = plane_shift(jnp.roll(coefficient, -depth_step, axis=-2), row_step, column_step)
        total = total + 0.5 * weight * (coefficient + other_coef) * (field - other)
    return total

def finish(sums):
    trace_vec = jnp.array([1.0, 1.0, 1.0, 0.0, 0.0, 0.0], jnp.float32)
    outer = trace_vec[:, None] * trace_vec[None, :]
    projector = jnp.eye(6, dtype=jnp.float32) - outer / 3.0
    tangent = sums[6] * outer + 2.0 * sums[7] * projector + 2.0 * sums[8:].reshape(6, 6)
    return jnp.concatenate([sums[:6], tangent.reshape(36)])

def one_rve(items):
    plastic, hardening, begin, delta, shear_field, bulk_field, yield_field, costs = items
    count = jnp.broadcast_to(costs.astype(jnp.float32)[:, None], (NBLK, BLK)).reshape(NZ, PLANE)
    stress, coefficient, plastic_new, hardening_new, weight, direction = return_map(plastic, hardening, begin, delta, shear_field, bulk_field, yield_field, count, SUBMAX)
    volume = float(NZ * PLANE)
    flat_direction = direction.reshape(6, NZ * PLANE)
    coupling = jnp.dot(weight.reshape(1, NZ * PLANE) * flat_direction, flat_direction.T, precision=lax.Precision.HIGHEST)
    sums = jnp.concatenate([lax.optimization_barrier(jnp.sum(stress, axis=(1, 2))), jnp.sum(bulk_field)[None], jnp.sum(coefficient)[None], coupling.reshape(36)]) / volume
    depth_diff = 0.5 * (jnp.roll(stress, -1, axis=-2) - jnp.roll(stress, 1, axis=-2))
    rhs = rhs_from(stress, depth_diff)
    solution = jnp.zeros_like(rhs)
    residual = rhs
    direction_cg = rhs
    norm_now = jnp.sum(residual * residual)
    for turn in range(ITERS):
        image = apply_operator(direction_cg, coefficient)
        alpha = norm_now / jnp.sum(direction_cg * image)
        solution = solution + alpha * direction_cg
        residual = residual - alpha * image
        norm_next = jnp.sum(residual * residual)
        direction_cg = residual + norm_next / norm_now * direction_cg
        norm_now = norm_next
    history = jnp.concatenate([plastic_new, hardening_new[None]], axis=0)
    return (solution, history, finish(sums))

def reference(plastic_strain, hardening_var, strain_start, strain_step, shear_mod, bulk_mod, yield_stress, substeps, pull_group, pull_block, owner):
    items = (jnp.moveaxis(plastic_strain, 1, 0), hardening_var, jnp.moveaxis(strain_start, 1, 0), jnp.moveaxis(strain_step, 1, 0), shear_mod, bulk_mod, yield_stress, substeps)
    solutions, histories, summaries = lax.map(one_rve, items)
    correction = jnp.moveaxis(solutions, 0, 1)
    blocks = histories.reshape(RVES, 7, NBLK, BLK)
    picked = blocks[pull_group, :, pull_block, :]
    inbox = jnp.transpose(picked, (2, 0, 1, 3))
    table = (owner[None, :] == jnp.arange(RVES)[:, None]).astype(jnp.float32)
    element_sums = jnp.dot(table, summaries, precision=lax.Precision.HIGHEST)
    return (correction, inbox, element_sums)
```

```python
import functools
import math

import jax
import jax.numpy as jnp
from jax import lax
from jax.experimental import pallas as pl
from jax.experimental.pallas import tpu as pltpu
from jax.sharding import PartitionSpec as P

NVX = 96
ITERS = 5
PLANE = 9216
BLK = 2304
LANES = 128
QUAD = 384
CHUNK = 1152
MESH = pl.DeviceIdType.MESH

hard_ratio = 0.3
mass_weight = 0.05
root_two_thirds = math.sqrt(2.0 / 3.0)
half_root = 1.0 / math.sqrt(2.0)
KEPT = (0, 1, 3, 4, 5)
PAIRS = tuple((i, j) for i in range(5) for j in range(i, 5))


def lane_id(rows):
    return lax.broadcasted_iota(jnp.int32, (rows, LANES), 1)


def unpack_rows(value):
    rows = value.shape[0]
    lane = lane_id(rows)
    a, b, c = value[:, 0:128], value[:, 128:256], value[:, 256:384]
    plain = (
        a,
        pltpu.roll(jnp.where(lane >= 96, a, b), 32, 1),
        pltpu.roll(jnp.where(lane >= 64, b, c), 64, 1),
        pltpu.roll(c, 96, 1),
    )
    out = []
    for row in plain:
        halo = jnp.where(lane < 112, pltpu.roll(row, 96, 1), pltpu.roll(row, 32, 1))
        out.append(jnp.where(lane < 96, row, halo))
    return out


def pack_rows(rows4):
    t0, t1, t2, t3 = rows4
    lane = lane_id(t0.shape[0])
    r1, r2, r3 = pltpu.roll(t1, 96, 1), pltpu.roll(t2, 64, 1), pltpu.roll(t3, 32, 1)
    return (
        jnp.where(lane < 96, t0, r1),
        jnp.where(lane < 64, r1, r2),
        jnp.where(lane < 32, r2, r3),
    )


def material_kernel(
    depth, volume, in_dev,
    sub_ref, pg_ref, pb_ref, p_ref, h_ref, b_ref, d_ref, g_ref, k_ref, y_ref,
    st_ref, pick_ref, sum_ref,
    acc_ref, hist_ref,
):
    step = pl.program_id(0)
    group = lax.axis_index("rve")
    slab = lax.axis_index("slab")
    groups = pg_ref.shape[0]
    per_block = BLK // CHUNK
    quarter = step // per_block
    blocks_dev = 4 * depth

    @pl.when(step == 0)
    def _():
        acc_ref[...] = jnp.zeros_like(acc_ref)

    zrow = lax.broadcasted_iota(jnp.int32, (depth, LANES), 0)
    count = jnp.zeros((depth, LANES), jnp.int32)
    turns = jnp.int32(1)
    for z in range(depth):
        n = sub_ref[group, slab * blocks_dev + z * 4 + quarter]
        count = jnp.where(zrow == z, n, count)
        turns = jnp.maximum(turns, n)
    count = jnp.concatenate([count] * (QUAD // LANES), axis=1)
    waiting = turns - count
    inv = 1.0 / count.astype(jnp.float32)
    waiting_f = waiting.astype(jnp.float32)

    def dev_parts(ref, lanes, other=None):
        parts = []
        for c in range(6):
            v = ref[c, 0, :, lanes]
            if other is not None:
                v = v - other[c, 0, :, lanes]
            parts.append(v)
        trace = parts[0] + parts[1] + parts[2]
        third = trace * (1.0 / 3.0)
        return [parts[c] - third if c < 3 else parts[c] for c in range(6)], trace

    def sub_chunk(sc, _):
        off = pl.multiple_of(sc * QUAD, QUAD)
        lanes = pl.ds(off, QUAD)
        dev0, tr0 = dev_parts(b_ref, lanes, p_ref)
        devs, trs = dev_parts(d_ref, lanes)
        mu = g_ref[0, :, lanes]
        hard = h_ref[0, :, lanes]
        delta = [devs[c] * inv for c in KEPT]
        start = [dev0[c] - waiting_f * delta[i] for i, c in enumerate(KEPT)]
        level0 = (11.0 * root_two_thirds / 2.2) * (y_ref[0, :, lanes] / mu + hard_ratio * hard)

        def trial(dd):
            dd = [dd[i] + delta[i] for i in range(5)]
            square = (
                2.0 * (dd[0] * (dd[0] + dd[1]) + dd[1] * dd[1])
                + dd[2] * dd[2] + dd[3] * dd[3] + dd[4] * dd[4]
            )
            square = jnp.maximum(square, 1e-30)
            return dd, square, lax.rsqrt(square)

        def substep(turn, carry):
            dd, level = carry
            dd, square, rs = trial(dd)
            fac = jnp.minimum((1.0 + level * rs) * (1.0 / 11.0), 1.0)
            fac = jnp.where(turn >= waiting, fac, 1.0)
            level = level + (1.0 - fac) * (square * rs)
            return tuple(fac * v for v in dd), level

        dd, level = lax.fori_loop(0, turns - 1, substep, (tuple(start), level0))
        dd, square, rs = trial(dd)
        fac = jnp.minimum((1.0 + level * rs) * (1.0 / 11.0), 1.0)
        level = level + (1.0 - fac) * (square * rs)
        fin = [fac * v for v in dd]
        coef = mu * fac
        weight = (coef - mu) * (rs * rs)
        bulk = k_ref[0, :, lanes]
        vol = bulk * (tr0 + trs)
        two_mu = 2.0 * mu
        ms = [two_mu * v for v in fin]
        wn = [weight * v for v in dd]
        terms = [vol, bulk, coef] + ms + [wn[i] * dd[j] for i, j in PAIRS]
        for t, v in enumerate(terms):
            acc_ref[t] += v[:, 0:128] + v[:, 128:256] + v[:, 256:384]
        ms6 = [ms[0], ms[1], -(ms[0] + ms[1]), ms[2], ms[3], ms[4]]
        fin6 = [fin[0], fin[1], -(fin[0] + fin[1]), fin[2], fin[3], fin[4]]
        fields = [ms6[c] + vol if c < 3 else ms6[c] for c in range(6)] + [coef]
        row0 = (step * (CHUNK // QUAD) + sc) * 4
        for f, v in enumerate(fields):
            for r, rowv in enumerate(unpack_rows(v)):
                for z0 in range(0, depth, 8):
                    nz = min(8, depth - z0)
                    st_ref[f, pl.ds(z0 * NVX + row0 + r, nz, stride=NVX), :] = rowv[z0 : z0 + nz]
        for c in range(6):
            hist_ref[c, :, lanes] = p_ref[c, 0, :, lanes] + (dev0[c] + devs[c] - fin6[c])
        hist_ref[6, :, lanes] = hard + root_two_thirds * (level - level0)
        return 0

    lax.fori_loop(0, CHUNK // QUAD, sub_chunk, 0)

    for g in range(groups):
        chosen = jnp.int32(0)
        for j in range(in_dev):
            slot = slab * in_dev + j
            chosen = jnp.where(
                pg_ref[g, slot] == group, pb_ref[g, slot] - slab * blocks_dev, chosen
            )

        @pl.when(chosen % 4 == quarter)
        def _():
            z = chosen // 4
            lanes = pl.ds(pl.multiple_of((step % per_block) * CHUNK, CHUNK), CHUNK)
            for c in range(7):
                pick_ref[g, pl.ds(c, 1), lanes] = hist_ref[c, pl.ds(z, 1), :]

    @pl.when(step == pl.num_programs(0) - 1)
    def _():
        tot = [
            jnp.sum(acc_ref[t], axis=(0, 1), keepdims=True) * (1.0 / volume)
            for t in range(8 + len(PAIRS))
        ]
        vol, bulk, coef = tot[0], tot[1], tot[2]
        ms = tot[3:8]
        stress = [vol + ms[0], vol + ms[1], vol - ms[0] - ms[1], ms[2], ms[3], ms[4]]
        table = {}
        for t, (i, j) in enumerate(PAIRS):
            table[(KEPT[i], KEPT[j])] = tot[8 + t]
            table[(KEPT[j], KEPT[i])] = tot[8 + t]
        for j in KEPT:
            table[(2, j)] = -(table[(0, j)] + table[(1, j)])
            table[(j, 2)] = table[(2, j)]
        table[(2, 2)] = -(table[(2, 0)] + table[(2, 1)])
        lane = lane_id(1)
        row = jnp.zeros((1, LANES), jnp.float32)
        for c in range(6):
            row = jnp.where(lane == c, stress[c], row)
        for i in range(6):
            for j in range(6):
                v = 2.0 * table[(i, j)]
                if i == j:
                    v = v + 2.0 * coef
                if i < 3 and j < 3:
                    v = v + bulk - (2.0 / 3.0) * coef
                row = jnp.where(lane == 6 + 6 * i + j, v, row)
        sum_ref[...] = row


def spread(v):
    p = v + pltpu.roll(v, NVX - 1, 0)
    p = p + pltpu.roll(p, 1, 0)
    q = p + pltpu.roll(p, LANES - 1, 1)
    return q + pltpu.roll(q, 1, 1)


def fold(v):
    out = v[0:8]
    for i in range(1, NVX // 8):
        out = out + v[8 * i : 8 * i + 8]
    return out


def solve_kernel(
    depth, groups, slabs, in_dev,
    pg_ref, own_ref, st_ref, pick_ref, sum_ref,
    out_ref, inbox_ref, elem_ref,
    sh, c8, ee, rr, im, al, dd, uu, hb, ps, red, ab, es, eo,
    nsend, nrecv, rsend, rrecv, bsend, brecv, esend, erecv,
):
    group = lax.axis_index("rve")
    slab = lax.axis_index("slab")
    up = lax.rem(slab + 1, slabs)
    down = lax.rem(slab + slabs - 1, slabs)
    last = depth - 1

    barrier = pltpu.get_barrier_semaphore()
    for k in range(1, slabs):
        pl.semaphore_signal(
            barrier, inc=1, device_id={"slab": lax.rem(slab + k, slabs)}, device_id_type=MESH
        )
    for k in range(1, groups):
        pl.semaphore_signal(
            barrier, inc=1, device_id={"rve": lax.rem(group + k, groups)}, device_id_type=MESH
        )
    pl.semaphore_wait(barrier, slabs + groups - 2)

    def remote(src, dst, ssem, rsem, axis, to):
        return pltpu.make_async_remote_copy(
            src_ref=src, dst_ref=dst, send_sem=ssem, recv_sem=rsem,
            device_id={axis: to}, device_id_type=MESH,
        )

    stress_up = remote(st_ref.at[:, last], sh.at[0], nsend.at[0, 0], nrecv.at[0, 0], "slab", up)
    stress_down = remote(st_ref.at[:, 0], sh.at[1], nsend.at[0, 1], nrecv.at[0, 1], "slab", down)
    stress_up.start()
    stress_down.start()
    moves = []
    for k in range(1, groups):
        to = lax.rem(group + k, groups)
        move = remote(pick_ref.at[to], ab.at[group], bsend.at[k], brecv.at[k], "rve", to)
        move.start()
        moves.append(move)

    c8[0] = jnp.zeros((NVX, LANES), jnp.float32)

    def own_planes(z, _):
        c8[z + 1] = st_ref[6, z] * 0.125
        return 0

    lax.fori_loop(0, depth, own_planes, 0)
    ab[group] = pick_ref[group]

    def ydiff(v):
        return pltpu.roll(v, NVX - 1, 0) - pltpu.roll(v, 1, 0)

    def xdiff(v):
        return pltpu.roll(v, LANES - 1, 1) - pltpu.roll(v, 1, 1)

    def rhs_plane(z, below, above):
        s3, s4, s5 = st_ref[3, z], st_ref[4, z], st_ref[5, z]
        zd = {c: above(c) - below(c) for c in (2, 3, 4)}
        hr = 0.5 * half_root
        v0 = 0.5 * xdiff(st_ref[0, z]) + hr * (ydiff(s5) + zd[4])
        v1 = hr * (xdiff(s5) + zd[3]) + 0.5 * ydiff(st_ref[1, z])
        v2 = hr * (xdiff(s4) + ydiff(s3)) + 0.5 * zd[2]
        for c, v in enumerate((v0, v1, v2)):
            rr[c, z + 1] = v

    def rhs_inner(z, _):
        rhs_plane(z, lambda c: st_ref[c, z - 1], lambda c: st_ref[c, z + 1])
        return 0

    lax.fori_loop(1, last, rhs_inner, 0)
    stress_up.wait()
    stress_down.wait()
    rhs_plane(0, lambda c: sh[0, c], lambda c: st_ref[c, 1])
    rhs_plane(last, lambda c: st_ref[c, last - 1], lambda c: sh[1, c])
    r_up = remote(rr.at[:, depth], rr.at[:, 0], nsend.at[1, 0], nrecv.at[1, 0], "slab", up)
    r_down = remote(rr.at[:, 1], rr.at[:, depth + 1], nsend.at[1, 1], nrecv.at[1, 1], "slab", down)
    r_up.start()
    r_down.start()
    c8[0] = sh[0, 6] * 0.125
    c8[depth + 1] = sh[1, 6] * 0.125

    def diagonal(z, _):
        ee[z] = 8.0 * (8.0 + mass_weight) * c8[z] + spread(c8[z - 1] + 2.0 * c8[z] + c8[z + 1])
        return 0

    lax.fori_loop(1, depth + 1, diagonal, 0)

    zero = jnp.zeros((8, LANES), jnp.float32)

    def apply_plane(z, carry):
        norm, curve = carry
        ca, cb, cc = c8[z - 1], c8[z], c8[z + 1]
        diag = ee[z]
        for c in range(3):
            ra, rb, rc = rr[c, z - 1], rr[c, z], rr[c, z + 1]
            crb = cb * rb
            plain = spread((ra + rc) + (rb + rb))
            mixed = spread((ca * ra + cc * rc) + (crb + crb))
            image = diag * rb - cb * plain - mixed
            im[c, z] = image
            norm = norm + fold(rb * rb)
            curve = curve + fold(rb * image)
        return norm, curve

    def reduce_start(it, norm, curve, extra):
        row = lax.broadcasted_iota(jnp.int32, (8, LANES), 0)
        n = jnp.sum(norm, axis=0, keepdims=True)
        c = jnp.sum(curve, axis=0, keepdims=True)
        tile = jnp.where(row == 0, n, jnp.where(row == 1, c, 0.0))
        if extra is not None:
            tile = jnp.where(row == 2, extra, tile)
        ps[it] = tile
        copies = []
        for k in range(1, slabs):
            to = lax.rem(slab + k, slabs)
            copy = remote(ps.at[it], red.at[it, slab], rsend.at[it, k], rrecv.at[it, k], "slab", to)
            copy.start()
            copies.append(copy)
        red[it, slab] = tile
        return copies

    def reduce_end(it, copies):
        for copy in copies:
            copy.wait()
        total = red[it, 0]
        for k in range(1, slabs):
            total = total + red[it, k]
        kept = jnp.where(lane_id(8) < NVX, total, 0.0)
        sums = jnp.sum(kept, axis=1, keepdims=True)
        return total, sums[0:1], sums[1:2]

    carry = lax.fori_loop(2, depth, apply_plane, (zero, zero))
    r_up.wait()
    r_down.wait()
    carry = apply_plane(1, carry)
    carry = apply_plane(depth, carry)

    def send_image(it):
        first = remote(im.at[:, depth], hb.at[it, 0], nsend.at[2 + it, 0], nrecv.at[2 + it, 0], "slab", up)
        second = remote(im.at[:, 1], hb.at[it, 1], nsend.at[2 + it, 1], nrecv.at[2 + it, 1], "slab", down)
        first.start()
        second.start()
        return first, second

    halos = send_image(0)
    copies = reduce_start(0, *carry, sum_ref[...])
    total, norm_now, curve_now = reduce_end(0, copies)
    eo[...] = total
    element = []
    for k in range(1, groups):
        to = lax.rem(group + k, groups)
        copy = remote(eo, es.at[group], esend.at[k], erecv.at[k], "rve", to)
        copy.start()
        element.append(copy)
    es[group] = total
    alpha = norm_now / curve_now

    ratio = None
    for turn in range(ITERS - 1):
        for copy in halos:
            copy.wait()

        def refresh(c, z, fresh):
            if turn > 0:
                fresh = fresh + ratio * al[c, z]
            al[c, z] = fresh
            rr[c, z] = rr[c, z] - alpha * fresh

        for c in range(3):
            refresh(c, 0, hb[turn, 0, c])
            refresh(c, depth + 1, hb[turn, 1, c])

        def direction(z):
            rows = pl.ds(pl.multiple_of((z - 1) * NVX, NVX), NVX)
            for c in range(3):
                if turn == 0:
                    d = rr[c, z]
                    uu[c, rows, :] = alpha * d
                else:
                    d = rr[c, z] + ratio * dd[c, z - 1]
                    uu[c, rows, :] = uu[c, rows, :] + alpha * d
                dd[c, z - 1] = d

        def update(z, _):
            direction(z)
            for c in range(3):
                refresh(c, z, im[c, z])
            return 0

        lax.fori_loop(1, depth + 1, update, 0)
        carry = apply_plane(1, (zero, zero))
        carry = apply_plane(depth, carry)
        if turn + 1 < ITERS - 1:
            halos = send_image(turn + 1)
        carry = lax.fori_loop(2, depth, apply_plane, carry)
        copies = reduce_start(turn + 1, *carry, None)
        _, norm_next, product = reduce_end(turn + 1, copies)
        ratio = norm_next / norm_now
        alpha = norm_next / (product - ratio * norm_next / alpha)
        norm_now = norm_next

    def last_turn(z, _):
        rows = pl.ds(pl.multiple_of(z * NVX, NVX), NVX)
        for c in range(3):
            d = rr[c, z + 1] + ratio * dd[c, z]
            uu[c, rows, :] = uu[c, rows, :] + alpha * d
        return 0

    lax.fori_loop(0, depth, last_turn, 0)

    def to_flat(j, _):
        for c in range(3):
            for z0 in range(0, depth, 8):
                nz = min(8, depth - z0)
                rows4 = [
                    uu[c, pl.ds(z0 * NVX + 4 * j + r, nz, stride=NVX), :] for r in range(4)
                ]
                for t, v in enumerate(pack_rows(rows4)):
                    off = pl.multiple_of(j * QUAD + t * LANES, LANES)
                    out_ref[c, 0, pl.ds(z0, nz), pl.ds(off, LANES)] = v
        return 0

    lax.fori_loop(0, PLANE // QUAD, to_flat, 0)

    for move in moves:
        move.wait()
    for j in range(in_dev):
        source = pg_ref[group, slab * in_dev + j]
        got = ab[source]
        for c in range(7):
            inbox_ref[c, 0, pl.ds(j, 1), :] = got[c : c + 1]
    for copy in element:
        copy.wait()
    mine = jnp.zeros((1, LANES), jnp.float32)
    for k in range(groups):
        mine = mine + jnp.where(own_ref[k] == group, es[k][2:3], 0.0)
    elem_ref[...] = mine[:, 0:42]


def on_device(
    groups, slabs,
    plastic_strain, hardening_var, strain_start, strain_step, shear_mod, bulk_mod, yield_stress,
    substeps, pull_group, pull_block, owner,
):
    depth = plastic_strain.shape[2]
    in_dev = pull_group.shape[1] // slabs
    volume = float(depth * slabs * PLANE)
    smem = pl.BlockSpec(memory_space=pltpu.SMEM)
    vmem = pl.BlockSpec(memory_space=pltpu.VMEM)
    f32 = jnp.float32
    six = pl.BlockSpec((6, 1, depth, CHUNK), lambda i: (0, 0, 0, i))
    one = pl.BlockSpec((1, depth, CHUNK), lambda i: (0, 0, i))

    def whole(shape):
        return pl.BlockSpec(shape, lambda i: (0,) * len(shape))

    shapes = ((7, depth * NVX, LANES), (groups, 7, BLK), (1, LANES))
    stress, picked, partial_sums = pl.pallas_call(
        functools.partial(material_kernel, depth, volume, in_dev),
        grid=(PLANE // CHUNK,),
        in_specs=[smem, smem, smem, six, one, six, six, one, one, one],
        out_specs=[whole(s) for s in shapes],
        out_shape=[jax.ShapeDtypeStruct(s, f32) for s in shapes],
        scratch_shapes=[
            pltpu.VMEM((8 + len(PAIRS), depth, LANES), f32),
            pltpu.VMEM((7, depth, CHUNK), f32),
        ],
        compiler_params=pltpu.CompilerParams(
            dimension_semantics=("arbitrary",), vmem_limit_bytes=48 * 1024 * 1024
        ),
        name="material",
    )(
        substeps, pull_group, pull_block, plastic_strain, hardening_var, strain_start,
        strain_step, shear_mod, bulk_mod, yield_stress,
    )
    stress = stress.reshape(7, depth, NVX, LANES)
    plane = (NVX, LANES)
    dma = pltpu.SemaphoreType.DMA
    correction, inbox, element_sums = pl.pallas_call(
        functools.partial(solve_kernel, depth, groups, slabs, in_dev),
        in_specs=[smem, smem, vmem, vmem, vmem],
        out_specs=[vmem, vmem, vmem],
        out_shape=[
            jax.ShapeDtypeStruct((3, 1, depth, PLANE), f32),
            jax.ShapeDtypeStruct((7, 1, in_dev, BLK), f32),
            jax.ShapeDtypeStruct((1, 42), f32),
        ],
        scratch_shapes=[
            pltpu.VMEM((2, 7) + plane, f32),
            pltpu.VMEM((depth + 2,) + plane, f32),
            pltpu.VMEM((depth + 2,) + plane, f32),
            pltpu.VMEM((3, depth + 2) + plane, f32),
            pltpu.VMEM((3, depth + 2) + plane, f32),
            pltpu.VMEM((3, depth + 2) + plane, f32),
            pltpu.VMEM((3, depth) + plane, f32),
            pltpu.VMEM((3, depth * NVX, LANES), f32),
            pltpu.VMEM((ITERS - 1, 2, 3) + plane, f32),
            pltpu.VMEM((ITERS, 8, LANES), f32),
            pltpu.VMEM((ITERS, slabs, 8, LANES), f32),
            pltpu.VMEM((groups, 7, BLK), f32),
            pltpu.VMEM((groups, 8, LANES), f32),
            pltpu.VMEM((8, LANES), f32),
            dma((ITERS + 1, 2)),
            dma((ITERS + 1, 2)),
            dma((ITERS, slabs)),
            dma((ITERS, slabs)),
            dma((groups,)),
            dma((groups,)),
            dma((groups,)),
            dma((groups,)),
        ],
        compiler_params=pltpu.CompilerParams(
            collective_id=0, has_side_effects=True, vmem_limit_bytes=60 * 1024 * 1024
        ),
        name="solve",
    )(pull_group, owner, stress, picked, partial_sums)
    return correction, inbox, element_sums


def solution(mesh):
    return jax.shard_map(
        functools.partial(on_device, mesh.shape["rve"], mesh.shape["slab"]),
        mesh=mesh,
        in_specs=(
            P(None, "rve", "slab", None),
            P("rve", "slab", None),
            P(None, "rve", "slab", None),
            P(None, "rve", "slab", None),
            P("rve", "slab", None),
            P("rve", "slab", None),
            P("rve", "slab", None),
            P(),
            P(),
            P(),
            P(),
        ),
        out_specs=(P(None, "rve", "slab", None), P(None, "rve", "slab", None), P("rve", None)),
        check_vma=False,
    )
```

```python
import functools
import math

import jax
import jax.numpy as jnp
from jax import lax
from jax.experimental import pallas as pl
from jax.experimental.pallas import tpu as pltpu
from jax.sharding import PartitionSpec as P

NVX = 96
ITERS = 5
PLANE = 9216
BLK = 2304
LANES = 128
PART = 24
MESH = pl.DeviceIdType.MESH

hard_ratio = 0.3
mass_weight = 0.05
root_two_thirds = math.sqrt(2.0 / 3.0)
half_root = 1.0 / math.sqrt(2.0)
KEPT = (0, 1, 3, 4, 5)
PAIRS = tuple((i, j) for i in range(5) for j in range(i, 5))


def lane_id(rows):
    return lax.broadcasted_iota(jnp.int32, (rows, LANES), 1)


def unpack_rows(a, b, c):
    lane = lane_id(a.shape[0])
    plain = (
        a,
        pltpu.roll(jnp.where(lane >= 96, a, b), 32, 1),
        pltpu.roll(jnp.where(lane >= 64, b, c), 64, 1),
        pltpu.roll(c, 96, 1),
    )
    out = []
    for row in plain:
        halo = jnp.where(lane < 112, pltpu.roll(row, 96, 1), pltpu.roll(row, 32, 1))
        out.append(jnp.where(lane < 96, row, halo))
    return out


def pack_rows(rows4):
    t0, t1, t2, t3 = rows4
    lane = lane_id(t0.shape[0])
    r1, r2, r3 = pltpu.roll(t1, 96, 1), pltpu.roll(t2, 64, 1), pltpu.roll(t3, 32, 1)
    return (
        jnp.where(lane < 96, t0, r1),
        jnp.where(lane < 64, r1, r2),
        jnp.where(lane < 32, r2, r3),
    )


def material_kernel(
    depth, volume, in_dev, planes,
    sub_ref, pg_ref, pb_ref, p_ref, h_ref, b_ref, d_ref, g_ref, k_ref, y_ref,
    st_ref, pick_ref, sum_ref,
    acc_ref, hist_ref, wait_ref, dev_ref, del_ref, lev_ref, lev0_ref, tmp_ref,
):
    step = pl.program_id(0)
    group = lax.axis_index("rve")
    slab = lax.axis_index("slab")
    groups = pg_ref.shape[0]
    blocks_dev = 4 * depth
    tiles = PLANE // LANES
    parts = tuple(slice(t, t + PART) for t in range(0, tiles, PART))
    quarter_rows = BLK // LANES

    @pl.when(step == 0)
    def _():
        acc_ref[...] = jnp.zeros_like(acc_ref)

    def dev_parts(ref, z, rows, other=None):
        vals = []
        for c in range(6):
            v = ref[c, z, rows]
            if other is not None:
                v = v - other[c, z, rows]
            vals.append(v)
        trace = vals[0] + vals[1] + vals[2]
        third = trace * (1.0 / 3.0)
        return [vals[c] - third if c < 3 else vals[c] for c in range(6)], trace

    def trial(rows):
        dd = [dev_ref[i, rows] + del_ref[i, rows] for i in range(5)]
        square = (
            2.0 * (dd[0] * (dd[0] + dd[1]) + dd[1] * dd[1])
            + dd[2] * dd[2] + dd[3] * dd[3] + dd[4] * dd[4]
        )
        square = jnp.maximum(square, 1e-30)
        return dd, square, lax.rsqrt(square)

    def one_plane(z, _):
        base = slab * blocks_dev + (step * planes + z) * 4
        counts = [sub_ref[group, base + q] for q in range(4)]
        turns = jnp.maximum(
            jnp.maximum(counts[0], counts[1]), jnp.maximum(counts[2], counts[3])
        )
        for rows in parts:
            row = lax.broadcasted_iota(jnp.int32, (PART, LANES), 0) + rows.start
            count = jnp.full((PART, LANES), counts[0], jnp.int32)
            for q in range(1, 4):
                count = jnp.where(row >= q * quarter_rows, counts[q], count)
            inv = 1.0 / count.astype(jnp.float32)
            waiting = turns - count
            wait_ref[rows] = waiting
            waiting_f = waiting.astype(jnp.float32)
            dev0, _ = dev_parts(b_ref, z, rows, p_ref)
            devs, _ = dev_parts(d_ref, z, rows)
            for i, c in enumerate(KEPT):
                delta = devs[c] * inv
                del_ref[i, rows] = delta
                dev_ref[i, rows] = dev0[c] - waiting_f * delta
            level0 = (11.0 * root_two_thirds / 2.2) * (
                y_ref[z, rows] / g_ref[z, rows] + hard_ratio * h_ref[z, rows]
            )
            lev_ref[rows] = level0
            lev0_ref[rows] = level0

        def substep(turn, _):
            for rows in parts:
                dd, square, rs = trial(rows)
                level = lev_ref[rows]
                fac = jnp.minimum((1.0 + level * rs) * (1.0 / 11.0), 1.0)
                fac = jnp.where(turn >= wait_ref[rows], fac, 1.0)
                lev_ref[rows] = level + (1.0 - fac) * (square * rs)
                for i in range(5):
                    dev_ref[i, rows] = fac * dd[i]
            return 0

        lax.fori_loop(0, turns - 1, substep, 0)
        sums = [None] * (8 + len(PAIRS))
        for rows in parts:
            dd, square, rs = trial(rows)
            level = lev_ref[rows]
            fac = jnp.minimum((1.0 + level * rs) * (1.0 / 11.0), 1.0)
            level = level + (1.0 - fac) * (square * rs)
            fin = [fac * v for v in dd]
            mu = g_ref[z, rows]
            coef = mu * fac
            weight = (coef - mu) * (rs * rs)
            bulk = k_ref[z, rows]
            dev0, tr0 = dev_parts(b_ref, z, rows, p_ref)
            devs, trs = dev_parts(d_ref, z, rows)
            vol = bulk * (tr0 + trs)
            two_mu = 2.0 * mu
            ms = [two_mu * v for v in fin]
            wn = [weight * v for v in dd]
            ms6 = [ms[0], ms[1], -(ms[0] + ms[1]), ms[2], ms[3], ms[4]]
            fin6 = [fin[0], fin[1], -(fin[0] + fin[1]), fin[2], fin[3], fin[4]]
            for c in range(6):
                tmp_ref[c, rows] = ms6[c] + vol if c < 3 else ms6[c]
                hist_ref[c, z, rows] = p_ref[c, z, rows] + (dev0[c] + devs[c] - fin6[c])
            tmp_ref[6, rows] = coef
            hist_ref[6, z, rows] = h_ref[z, rows] + root_two_thirds * (level - lev0_ref[rows])
            terms = [vol, bulk, coef] + ms + [wn[i] * dd[j] for i, j in PAIRS]
            for t, v in enumerate(terms):
                for o in range(0, PART, 8):
                    piece = v[o : o + 8]
                    sums[t] = piece if sums[t] is None else sums[t] + piece
        for t, v in enumerate(sums):
            acc_ref[t] += v

        for f in range(7):
            for g8 in range(tiles // 24):
                a, b, c = (tmp_ref[f, pl.ds(24 * g8 + k, 8, stride=3)] for k in range(3))
                for r, rowv in enumerate(unpack_rows(a, b, c)):
                    st_ref[f, z, pl.ds(32 * g8 + r, 8, stride=4)] = rowv
        return 0

    lax.fori_loop(0, planes, one_plane, 0)

    for g in range(groups):
        chosen = jnp.int32(0)
        for j in range(in_dev):
            slot = slab * in_dev + j
            chosen = jnp.where(
                pg_ref[g, slot] == group, pb_ref[g, slot] - slab * blocks_dev, chosen
            )
        z = chosen // 4 - step * planes

        @pl.when((z >= 0) & (z < planes))
        def _():
            for q in range(4):

                @pl.when(chosen % 4 == q)
                def _():
                    for c in range(7):
                        pick_ref[g, c] = hist_ref[c, z, q * quarter_rows : (q + 1) * quarter_rows]

    @pl.when(step == pl.num_programs(0) - 1)
    def _():
        tot = [
            jnp.sum(acc_ref[t], axis=(0, 1), keepdims=True) * (1.0 / volume)
            for t in range(8 + len(PAIRS))
        ]
        vol, bulk, coef = tot[0], tot[1], tot[2]
        ms = tot[3:8]
        stress = [vol + ms[0], vol + ms[1], vol - ms[0] - ms[1], ms[2], ms[3], ms[4]]
        table = {}
        for t, (i, j) in enumerate(PAIRS):
            table[(KEPT[i], KEPT[j])] = tot[8 + t]
            table[(KEPT[j], KEPT[i])] = tot[8 + t]
        for j in KEPT:
            table[(2, j)] = -(table[(0, j)] + table[(1, j)])
            table[(j, 2)] = table[(2, j)]
        table[(2, 2)] = -(table[(2, 0)] + table[(2, 1)])
        lane = lane_id(1)
        row = jnp.zeros((1, LANES), jnp.float32)
        for c in range(6):
            row = jnp.where(lane == c, stress[c], row)
        for i in range(6):
            for j in range(6):
                v = 2.0 * table[(i, j)]
                if i == j:
                    v = v + 2.0 * coef
                if i < 3 and j < 3:
                    v = v + bulk - (2.0 / 3.0) * coef
                row = jnp.where(lane == 6 + 6 * i + j, v, row)
        sum_ref[...] = row


def spread(v):
    p = v + pltpu.roll(v, NVX - 1, 0)
    p = p + pltpu.roll(p, 1, 0)
    q = p + pltpu.roll(p, LANES - 1, 1)
    return q + pltpu.roll(q, 1, 1)


def fold(v):
    out = v[0:8]
    for i in range(1, NVX // 8):
        out = out + v[8 * i : 8 * i + 8]
    return out


def solve_kernel(
    depth, groups, slabs, in_dev,
    pg_ref, own_ref, st_ref, pick_ref, sum_ref,
    out_ref, inbox_ref, elem_ref,
    sh, c8, ee, rr, im, al, dd, uu, hb, ps, red, ab, es, eo,
    nsend, nrecv, rsend, rrecv, bsend, brecv, esend, erecv,
):
    group = lax.axis_index("rve")
    slab = lax.axis_index("slab")
    up = lax.rem(slab + 1, slabs)
    down = lax.rem(slab + slabs - 1, slabs)
    last = depth - 1

    barrier = pltpu.get_barrier_semaphore()
    for k in range(1, slabs):
        pl.semaphore_signal(
            barrier, inc=1, device_id={"slab": lax.rem(slab + k, slabs)}, device_id_type=MESH
        )
    for k in range(1, groups):
        pl.semaphore_signal(
            barrier, inc=1, device_id={"rve": lax.rem(group + k, groups)}, device_id_type=MESH
        )
    pl.semaphore_wait(barrier, slabs + groups - 2)

    def remote(src, dst, ssem, rsem, axis, to):
        return pltpu.make_async_remote_copy(
            src_ref=src, dst_ref=dst, send_sem=ssem, recv_sem=rsem,
            device_id={axis: to}, device_id_type=MESH,
        )

    stress_up = remote(st_ref.at[:, last], sh.at[0], nsend.at[0, 0], nrecv.at[0, 0], "slab", up)
    stress_down = remote(st_ref.at[:, 0], sh.at[1], nsend.at[0, 1], nrecv.at[0, 1], "slab", down)
    stress_up.start()
    stress_down.start()
    moves = []
    for k in range(1, groups):
        to = lax.rem(group + k, groups)
        move = remote(pick_ref.at[to], ab.at[group], bsend.at[k], brecv.at[k], "rve", to)
        move.start()
        moves.append(move)

    def own_planes(z, _):
        c8[z + 1] = st_ref[6, z] * 0.125
        return 0

    lax.fori_loop(0, depth, own_planes, 0)
    ab[group] = pick_ref[group]

    def ydiff(v):
        return pltpu.roll(v, NVX - 1, 0) - pltpu.roll(v, 1, 0)

    def xdiff(v):
        return pltpu.roll(v, LANES - 1, 1) - pltpu.roll(v, 1, 1)

    def rhs_plane(z, below, above):
        s3, s4, s5 = st_ref[3, z], st_ref[4, z], st_ref[5, z]
        zd = {c: above(c) - below(c) for c in (2, 3, 4)}
        hr = 0.5 * half_root
        v0 = 0.5 * xdiff(st_ref[0, z]) + hr * (ydiff(s5) + zd[4])
        v1 = hr * (xdiff(s5) + zd[3]) + 0.5 * ydiff(st_ref[1, z])
        v2 = hr * (xdiff(s4) + ydiff(s3)) + 0.5 * zd[2]
        for c, v in enumerate((v0, v1, v2)):
            rr[c, z + 1] = v

    def rhs_inner(z, _):
        rhs_plane(z, lambda c: st_ref[c, z - 1], lambda c: st_ref[c, z + 1])
        return 0

    lax.fori_loop(1, last, rhs_inner, 0)
    stress_up.wait()
    stress_down.wait()
    rhs_plane(0, lambda c: sh[0, c], lambda c: st_ref[c, 1])
    rhs_plane(last, lambda c: st_ref[c, last - 1], lambda c: sh[1, c])
    r_up = remote(rr.at[:, depth], rr.at[:, 0], nsend.at[1, 0], nrecv.at[1, 0], "slab", up)
    r_down = remote(rr.at[:, 1], rr.at[:, depth + 1], nsend.at[1, 1], nrecv.at[1, 1], "slab", down)
    r_up.start()
    r_down.start()
    c8[0] = sh[0, 6] * 0.125
    c8[depth + 1] = sh[1, 6] * 0.125

    def diagonal(z, _):
        ee[z] = 8.0 * (8.0 + mass_weight) * c8[z] + spread(c8[z - 1] + 2.0 * c8[z] + c8[z + 1])
        return 0

    lax.fori_loop(1, depth + 1, diagonal, 0)

    zero = jnp.zeros((8, LANES), jnp.float32)

    def apply_plane(z, carry):
        norm, curve = carry
        ca, cb, cc = c8[z - 1], c8[z], c8[z + 1]
        diag = ee[z]
        for c in range(3):
            ra, rb, rc = rr[c, z - 1], rr[c, z], rr[c, z + 1]
            crb = cb * rb
            plain = spread((ra + rc) + (rb + rb))
            mixed = spread((ca * ra + cc * rc) + (crb + crb))
            image = diag * rb - cb * plain - mixed
            im[c, z] = image
            norm = norm + fold(rb * rb)
            curve = curve + fold(rb * image)
        return norm, curve

    def reduce_start(it, norm, curve, extra):
        row = lax.broadcasted_iota(jnp.int32, (8, LANES), 0)
        n = jnp.sum(norm, axis=0, keepdims=True)
        c = jnp.sum(curve, axis=0, keepdims=True)
        tile = jnp.where(row == 0, n, jnp.where(row == 1, c, 0.0))
        if extra is not None:
            tile = jnp.where(row == 2, extra, tile)
        ps[it] = tile
        copies = []
        for k in range(1, slabs):
            to = lax.rem(slab + k, slabs)
            copy = remote(ps.at[it], red.at[it, slab], rsend.at[it, k], rrecv.at[it, k], "slab", to)
            copy.start()
            copies.append(copy)
        red[it, slab] = tile
        return copies

    def reduce_end(it, copies):
        for copy in copies:
            copy.wait()
        total = red[it, 0]
        for k in range(1, slabs):
            total = total + red[it, k]
        kept = jnp.where(lane_id(8) < NVX, total, 0.0)
        sums = jnp.sum(kept, axis=1, keepdims=True)
        return total, sums[0:1], sums[1:2]

    carry = lax.fori_loop(2, depth, apply_plane, (zero, zero))
    r_up.wait()
    r_down.wait()
    carry = apply_plane(1, carry)
    carry = apply_plane(depth, carry)

    def send_image(it):
        first = remote(im.at[:, depth], hb.at[it, 0], nsend.at[2 + it, 0], nrecv.at[2 + it, 0], "slab", up)
        second = remote(im.at[:, 1], hb.at[it, 1], nsend.at[2 + it, 1], nrecv.at[2 + it, 1], "slab", down)
        first.start()
        second.start()
        return first, second

    halos = send_image(0)
    copies = reduce_start(0, *carry, sum_ref[...])
    total, norm_now, curve_now = reduce_end(0, copies)
    eo[...] = total
    element = []
    for k in range(1, groups):
        to = lax.rem(group + k, groups)
        copy = remote(eo, es.at[group], esend.at[k], erecv.at[k], "rve", to)
        copy.start()
        element.append(copy)
    es[group] = total
    alpha = norm_now / curve_now

    ratio = None
    for turn in range(ITERS - 1):
        for copy in halos:
            copy.wait()

        def refresh(c, z, fresh):
            if turn > 0:
                fresh = fresh + ratio * al[c, z]
            al[c, z] = fresh
            rr[c, z] = rr[c, z] - alpha * fresh

        for c in range(3):
            refresh(c, 0, hb[turn, 0, c])
            refresh(c, depth + 1, hb[turn, 1, c])

        def direction(z):
            rows = pl.ds(pl.multiple_of((z - 1) * NVX, NVX), NVX)
            for c in range(3):
                if turn == 0:
                    d = rr[c, z]
                    uu[c, rows, :] = alpha * d
                else:
                    d = rr[c, z] + ratio * dd[c, z - 1]
                    uu[c, rows, :] = uu[c, rows, :] + alpha * d
                dd[c, z - 1] = d

        def update(z, _):
            direction(z)
            for c in range(3):
                refresh(c, z, im[c, z])
            return 0

        lax.fori_loop(1, depth + 1, update, 0)
        carry = apply_plane(1, (zero, zero))
        carry = apply_plane(depth, carry)
        if turn + 1 < ITERS - 1:
            halos = send_image(turn + 1)
        carry = lax.fori_loop(2, depth, apply_plane, carry)
        copies = reduce_start(turn + 1, *carry, None)
        _, norm_next, product = reduce_end(turn + 1, copies)
        ratio = norm_next / norm_now
        alpha = norm_next / (product - ratio * norm_next / alpha)
        norm_now = norm_next

    def last_turn(z, _):
        rows = pl.ds(pl.multiple_of(z * NVX, NVX), NVX)
        for c in range(3):
            d = rr[c, z + 1] + ratio * dd[c, z]
            uu[c, rows, :] = uu[c, rows, :] + alpha * d
        return 0

    lax.fori_loop(0, depth, last_turn, 0)

    def to_flat(z, _):
        for c in range(3):
            for g8 in range(NVX // 32):
                rows4 = [
                    uu[c, pl.ds(z * NVX + 32 * g8 + r, 8, stride=4), :] for r in range(4)
                ]
                for t, v in enumerate(pack_rows(rows4)):
                    out_ref[c, z, pl.ds(24 * g8 + t, 8, stride=3)] = v
        return 0

    lax.fori_loop(0, depth, to_flat, 0)

    for move in moves:
        move.wait()
    for j in range(in_dev):
        source = pg_ref[group, slab * in_dev + j]
        got = ab[source]
        for c in range(7):
            inbox_ref[c, pl.ds(j, BLK // LANES, stride=in_dev), :] = got[c]
    for copy in element:
        copy.wait()
    mine = jnp.zeros((1, LANES), jnp.float32)
    for k in range(groups):
        mine = mine + jnp.where(own_ref[k] == group, es[k][2:3], 0.0)
    elem_ref[...] = mine[:, 0:42]


def on_device(
    groups, slabs,
    plastic_strain, hardening_var, strain_start, strain_step, shear_mod, bulk_mod, yield_stress,
    substeps, pull_group, pull_block, owner,
):
    depth = plastic_strain.shape[2]
    in_dev = pull_group.shape[1] // slabs
    volume = float(depth * slabs * PLANE)
    smem = pl.BlockSpec(memory_space=pltpu.SMEM)
    vmem = pl.BlockSpec(memory_space=pltpu.VMEM)
    f32 = jnp.float32
    tiles = PLANE // LANES
    planes = depth // 4 if depth % 4 == 0 else 1
    six = pl.BlockSpec((6, planes, tiles, LANES), lambda i: (0, i, 0, 0))
    one = pl.BlockSpec((planes, tiles, LANES), lambda i: (i, 0, 0))

    def whole(shape):
        return pl.BlockSpec(shape, lambda i: (0,) * len(shape))

    def view6(x):
        return x.reshape(6, depth, tiles, LANES)

    def view1(x):
        return x.reshape(depth, tiles, LANES)

    pick_shape = (groups, 7, BLK // LANES, LANES)
    shapes = ((7, depth, NVX, LANES), pick_shape, (1, LANES))
    stress, picked, partial_sums = pl.pallas_call(
        functools.partial(material_kernel, depth, volume, in_dev, planes),
        grid=(depth // planes,),
        in_specs=[smem, smem, smem, six, one, six, six, one, one, one],
        out_specs=[
            pl.BlockSpec((7, planes, NVX, LANES), lambda i: (0, i, 0, 0)),
            whole(shapes[1]),
            whole(shapes[2]),
        ],
        out_shape=[jax.ShapeDtypeStruct(s, f32) for s in shapes],
        scratch_shapes=[
            pltpu.VMEM((8 + len(PAIRS), 8, LANES), f32),
            pltpu.VMEM((7, planes, tiles, LANES), f32),
            pltpu.VMEM((tiles, LANES), jnp.int32),
            pltpu.VMEM((5, tiles, LANES), f32),
            pltpu.VMEM((5, tiles, LANES), f32),
            pltpu.VMEM((tiles, LANES), f32),
            pltpu.VMEM((tiles, LANES), f32),
            pltpu.VMEM((7, tiles, LANES), f32),
        ],
        compiler_params=pltpu.CompilerParams(
            dimension_semantics=("arbitrary",), vmem_limit_bytes=16 * 1024 * 1024
        ),
        name="material",
    )(
        substeps, pull_group, pull_block, view6(plastic_strain), view1(hardening_var),
        view6(strain_start), view6(strain_step), view1(shear_mod), view1(bulk_mod),
        view1(yield_stress),
    )
    plane = (NVX, LANES)
    dma = pltpu.SemaphoreType.DMA
    correction, inbox, element_sums = pl.pallas_call(
        functools.partial(solve_kernel, depth, groups, slabs, in_dev),
        in_specs=[smem, smem, vmem, vmem, vmem],
        out_specs=[vmem, vmem, vmem],
        out_shape=[
            jax.ShapeDtypeStruct((3, depth, tiles, LANES), f32),
            jax.ShapeDtypeStruct((7, in_dev * BLK // LANES, LANES), f32),
            jax.ShapeDtypeStruct((1, 42), f32),
        ],
        scratch_shapes=[
            pltpu.VMEM((2, 7) + plane, f32),
            pltpu.VMEM((depth + 2,) + plane, f32),
            pltpu.VMEM((depth + 2,) + plane, f32),
            pltpu.VMEM((3, depth + 2) + plane, f32),
            pltpu.VMEM((3, depth + 2) + plane, f32),
            pltpu.VMEM((3, depth + 2) + plane, f32),
            pltpu.VMEM((3, depth) + plane, f32),
            pltpu.VMEM((3, depth * NVX, LANES), f32),
            pltpu.VMEM((ITERS - 1, 2, 3) + plane, f32),
            pltpu.VMEM((ITERS, 8, LANES), f32),
            pltpu.VMEM((ITERS, slabs, 8, LANES), f32),
            pltpu.VMEM(pick_shape, f32),
            pltpu.VMEM((groups, 8, LANES), f32),
            pltpu.VMEM((8, LANES), f32),
            dma((ITERS + 1, 2)),
            dma((ITERS + 1, 2)),
            dma((ITERS, slabs)),
            dma((ITERS, slabs)),
            dma((groups,)),
            dma((groups,)),
            dma((groups,)),
            dma((groups,)),
        ],
        compiler_params=pltpu.CompilerParams(
            collective_id=0, has_side_effects=True, vmem_limit_bytes=26 * 1024 * 1024
        ),
        name="solve",
    )(pull_group, owner, stress, picked, partial_sums)
    correction = correction.reshape(3, 1, depth, PLANE)
    inbox = inbox.reshape(7, BLK // LANES, in_dev, LANES).swapaxes(1, 2)
    return correction, inbox.reshape(7, 1, in_dev, BLK), element_sums


def solution(mesh):
    return jax.shard_map(
        functools.partial(on_device, mesh.shape["rve"], mesh.shape["slab"]),
        mesh=mesh,
        in_specs=(
            P(None, "rve", "slab", None),
            P("rve", "slab", None),
            P(None, "rve", "slab", None),
            P(None, "rve", "slab", None),
            P("rve", "slab", None),
            P("rve", "slab", None),
            P("rve", "slab", None),
            P(),
            P(),
            P(),
            P(),
        ),
        out_specs=(P(None, "rve", "slab", None), P(None, "rve", "slab", None), P("rve", None)),
        check_vma=False,
    )
```

```python
import functools
import math

import jax
import jax.numpy as jnp
from jax import lax
from jax.experimental import pallas as pl
from jax.experimental.pallas import tpu as pltpu
from jax.sharding import PartitionSpec as P

NVX = 96
ITERS = 5
PLANE = 9216
BLK = 2304
LANES = 128
PART = 24
MESH = pl.DeviceIdType.MESH

hard_ratio = 0.3
mass_weight = 0.05
root_two_thirds = math.sqrt(2.0 / 3.0)
half_root = 1.0 / math.sqrt(2.0)
KEPT = (0, 1, 3, 4, 5)
PAIRS = tuple((i, j) for i in range(5) for j in range(i, 5))


def lane_id(rows):
    return lax.broadcasted_iota(jnp.int32, (rows, LANES), 1)


def unpack_rows(a, b, c):
    lane = lane_id(a.shape[0])
    plain = (
        a,
        pltpu.roll(jnp.where(lane >= 96, a, b), 32, 1),
        pltpu.roll(jnp.where(lane >= 64, b, c), 64, 1),
        pltpu.roll(c, 96, 1),
    )
    out = []
    for row in plain:
        halo = jnp.where(lane < 112, pltpu.roll(row, 96, 1), pltpu.roll(row, 32, 1))
        out.append(jnp.where(lane < 96, row, halo))
    return out


def pack_rows(rows4):
    t0, t1, t2, t3 = rows4
    lane = lane_id(t0.shape[0])
    r1, r2, r3 = pltpu.roll(t1, 96, 1), pltpu.roll(t2, 64, 1), pltpu.roll(t3, 32, 1)
    return (
        jnp.where(lane < 96, t0, r1),
        jnp.where(lane < 64, r1, r2),
        jnp.where(lane < 32, r2, r3),
    )


def material_kernel(
    depth, volume, in_dev, planes,
    sub_ref, pg_ref, pb_ref, p_ref, h_ref, b_ref, d_ref, g_ref, k_ref, y_ref,
    st_ref, pick_ref, sum_ref,
    acc_ref, hist_ref, wait_ref, dev_ref, del_ref, lev_ref, lev0_ref, tmp_ref,
):
    step = pl.program_id(0)
    group = lax.axis_index("rve")
    slab = lax.axis_index("slab")
    groups = pg_ref.shape[0]
    blocks_dev = 4 * depth
    tiles = PLANE // LANES
    parts = tuple(slice(t, t + PART) for t in range(0, tiles, PART))
    quarter_rows = BLK // LANES

    @pl.when(step == 0)
    def _():
        acc_ref[...] = jnp.zeros_like(acc_ref)

    def dev_parts(ref, z, rows, other=None):
        vals = []
        for c in range(6):
            v = ref[c, z, rows]
            if other is not None:
                v = v - other[c, z, rows]
            vals.append(v)
        trace = vals[0] + vals[1] + vals[2]
        third = trace * (1.0 / 3.0)
        return [vals[c] - third if c < 3 else vals[c] for c in range(6)], trace

    def trial(rows):
        dd = [dev_ref[i, rows] + del_ref[i, rows] for i in range(5)]
        square = (
            2.0 * (dd[0] * (dd[0] + dd[1]) + dd[1] * dd[1])
            + dd[2] * dd[2] + dd[3] * dd[3] + dd[4] * dd[4]
        )
        square = jnp.maximum(square, 1e-30)
        return dd, square, lax.rsqrt(square)

    def one_plane(z, _):
        base = slab * blocks_dev + (step * planes + z) * 4
        counts = [sub_ref[group, base + q] for q in range(4)]
        turns = jnp.maximum(
            jnp.maximum(counts[0], counts[1]), jnp.maximum(counts[2], counts[3])
        )
        for rows in parts:
            row = lax.broadcasted_iota(jnp.int32, (PART, LANES), 0) + rows.start
            count = jnp.full((PART, LANES), counts[0], jnp.int32)
            for q in range(1, 4):
                count = jnp.where(row >= q * quarter_rows, counts[q], count)
            inv = 1.0 / count.astype(jnp.float32)
            waiting = turns - count
            wait_ref[rows] = waiting
            waiting_f = waiting.astype(jnp.float32)
            dev0, _ = dev_parts(b_ref, z, rows, p_ref)
            devs, _ = dev_parts(d_ref, z, rows)
            for i, c in enumerate(KEPT):
                delta = devs[c] * inv
                del_ref[i, rows] = delta
                dev_ref[i, rows] = dev0[c] - waiting_f * delta
            level0 = (11.0 * root_two_thirds / 2.2) * (
                y_ref[z, rows] / g_ref[z, rows] + hard_ratio * h_ref[z, rows]
            )
            lev_ref[rows] = level0
            lev0_ref[rows] = level0

        def substep(turn, _):
            for rows in parts:
                dd, square, rs = trial(rows)
                level = lev_ref[rows]
                fac = jnp.minimum((1.0 + level * rs) * (1.0 / 11.0), 1.0)
                fac = jnp.where(turn >= wait_ref[rows], fac, 1.0)
                lev_ref[rows] = level + (1.0 - fac) * (square * rs)
                for i in range(5):
                    dev_ref[i, rows] = fac * dd[i]
            return 0

        lax.fori_loop(0, turns - 1, substep, 0)
        sums = [None] * (8 + len(PAIRS))
        for rows in parts:
            dd, square, rs = trial(rows)
            level = lev_ref[rows]
            fac = jnp.minimum((1.0 + level * rs) * (1.0 / 11.0), 1.0)
            level = level + (1.0 - fac) * (square * rs)
            fin = [fac * v for v in dd]
            mu = g_ref[z, rows]
            coef = mu * fac
            weight = (coef - mu) * (rs * rs)
            bulk = k_ref[z, rows]
            dev0, tr0 = dev_parts(b_ref, z, rows, p_ref)
            devs, trs = dev_parts(d_ref, z, rows)
            vol = bulk * (tr0 + trs)
            two_mu = 2.0 * mu
            ms = [two_mu * v for v in fin]
            wn = [weight * v for v in dd]
            ms6 = [ms[0], ms[1], -(ms[0] + ms[1]), ms[2], ms[3], ms[4]]
            fin6 = [fin[0], fin[1], -(fin[0] + fin[1]), fin[2], fin[3], fin[4]]
            for c in range(6):
                tmp_ref[c, rows] = ms6[c] + vol if c < 3 else ms6[c]
                hist_ref[c, z, rows] = p_ref[c, z, rows] + (dev0[c] + devs[c] - fin6[c])
            tmp_ref[6, rows] = coef
            hist_ref[6, z, rows] = h_ref[z, rows] + root_two_thirds * (level - lev0_ref[rows])
            terms = [vol, bulk, coef] + ms + [wn[i] * dd[j] for i, j in PAIRS]
            for t, v in enumerate(terms):
                for o in range(0, PART, 8):
                    piece = v[o : o + 8]
                    sums[t] = piece if sums[t] is None else sums[t] + piece
        for t, v in enumerate(sums):
            acc_ref[t] += v

        for f in range(7):
            for g8 in range(tiles // 24):
                a, b, c = (tmp_ref[f, pl.ds(24 * g8 + k, 8, stride=3)] for k in range(3))
                for r, rowv in enumerate(unpack_rows(a, b, c)):
                    st_ref[f, z, pl.ds(32 * g8 + r, 8, stride=4)] = rowv
        return 0

    lax.fori_loop(0, planes, one_plane, 0)

    for g in range(groups):
        chosen = jnp.int32(0)
        for j in range(in_dev):
            slot = slab * in_dev + j
            chosen = jnp.where(
                pg_ref[g, slot] == group, pb_ref[g, slot] - slab * blocks_dev, chosen
            )
        z = chosen // 4 - step * planes

        @pl.when((z >= 0) & (z < planes))
        def _():
            for q in range(4):

                @pl.when(chosen % 4 == q)
                def _():
                    for c in range(7):
                        pick_ref[g, c] = hist_ref[c, z, q * quarter_rows : (q + 1) * quarter_rows]

    @pl.when(step == pl.num_programs(0) - 1)
    def _():
        tot = [
            jnp.sum(acc_ref[t], axis=(0, 1), keepdims=True) * (1.0 / volume)
            for t in range(8 + len(PAIRS))
        ]
        vol, bulk, coef = tot[0], tot[1], tot[2]
        ms = tot[3:8]
        stress = [vol + ms[0], vol + ms[1], vol - ms[0] - ms[1], ms[2], ms[3], ms[4]]
        table = {}
        for t, (i, j) in enumerate(PAIRS):
            table[(KEPT[i], KEPT[j])] = tot[8 + t]
            table[(KEPT[j], KEPT[i])] = tot[8 + t]
        for j in KEPT:
            table[(2, j)] = -(table[(0, j)] + table[(1, j)])
            table[(j, 2)] = table[(2, j)]
        table[(2, 2)] = -(table[(2, 0)] + table[(2, 1)])
        lane = lane_id(1)
        row = jnp.zeros((1, LANES), jnp.float32)
        for c in range(6):
            row = jnp.where(lane == c, stress[c], row)
        for i in range(6):
            for j in range(6):
                v = 2.0 * table[(i, j)]
                if i == j:
                    v = v + 2.0 * coef
                if i < 3 and j < 3:
                    v = v + bulk - (2.0 / 3.0) * coef
                row = jnp.where(lane == 6 + 6 * i + j, v, row)
        sum_ref[...] = row


def ring_next(pieces, sub):
    turned = [pltpu.roll(p, 7, 0) for p in pieces]
    count = len(pieces)
    return [jnp.where(sub < 7, turned[i], turned[(i + 1) % count]) for i in range(count)]


def ring_prev(pieces, sub):
    turned = [pltpu.roll(p, 1, 0) for p in pieces]
    count = len(pieces)
    return [jnp.where(sub > 0, turned[i], turned[i - 1]) for i in range(count)]


def cut(v):
    return [v[i : i + 8] for i in range(0, NVX, 8)]


def spread(pieces, sub):
    p = [x + y for x, y in zip(pieces, ring_next(pieces, sub))]
    p = [x + y for x, y in zip(p, ring_prev(p, sub))]
    q = [x + pltpu.roll(x, LANES - 1, 1) for x in p]
    return [x + pltpu.roll(x, 1, 1) for x in q]


def solve_kernel(
    depth, groups, slabs, in_dev,
    pg_ref, own_ref, st_ref, pick_ref, sum_ref,
    out_ref, inbox_ref, elem_ref,
    sh, c8, ee, rr, im, al, dd, uu, hb, ps, red, ab, es, eo,
    nsend, nrecv, rsend, rrecv, bsend, brecv, esend, erecv,
):
    group = lax.axis_index("rve")
    slab = lax.axis_index("slab")
    up = lax.rem(slab + 1, slabs)
    down = lax.rem(slab + slabs - 1, slabs)
    last = depth - 1

    barrier = pltpu.get_barrier_semaphore()
    for k in range(1, slabs):
        pl.semaphore_signal(
            barrier, inc=1, device_id={"slab": lax.rem(slab + k, slabs)}, device_id_type=MESH
        )
    for k in range(1, groups):
        pl.semaphore_signal(
            barrier, inc=1, device_id={"rve": lax.rem(group + k, groups)}, device_id_type=MESH
        )
    pl.semaphore_wait(barrier, slabs + groups - 2)

    def remote(src, dst, ssem, rsem, axis, to):
        return pltpu.make_async_remote_copy(
            src_ref=src, dst_ref=dst, send_sem=ssem, recv_sem=rsem,
            device_id={axis: to}, device_id_type=MESH,
        )

    stress_up = remote(st_ref.at[:, last], sh.at[0], nsend.at[0, 0], nrecv.at[0, 0], "slab", up)
    stress_down = remote(st_ref.at[:, 0], sh.at[1], nsend.at[0, 1], nrecv.at[0, 1], "slab", down)
    stress_up.start()
    stress_down.start()
    moves = []
    for k in range(1, groups):
        to = lax.rem(group + k, groups)
        move = remote(pick_ref.at[to], ab.at[group], bsend.at[k], brecv.at[k], "rve", to)
        move.start()
        moves.append(move)

    def own_planes(z, _):
        c8[z + 1] = st_ref[6, z] * 0.125
        return 0

    lax.fori_loop(0, depth, own_planes, 0)
    ab[group] = pick_ref[group]

    sub = lax.broadcasted_iota(jnp.int32, (8, LANES), 0)

    def ydiff(v):
        v = cut(v)
        both = [x - y for x, y in zip(ring_next(v, sub), ring_prev(v, sub))]
        return jnp.concatenate(both, axis=0)

    def xdiff(v):
        return pltpu.roll(v, LANES - 1, 1) - pltpu.roll(v, 1, 1)

    def rhs_plane(z, below, above):
        s3, s4, s5 = st_ref[3, z], st_ref[4, z], st_ref[5, z]
        zd = {c: above(c) - below(c) for c in (2, 3, 4)}
        hr = 0.5 * half_root
        v0 = 0.5 * xdiff(st_ref[0, z]) + hr * (ydiff(s5) + zd[4])
        v1 = hr * (xdiff(s5) + zd[3]) + 0.5 * ydiff(st_ref[1, z])
        v2 = hr * (xdiff(s4) + ydiff(s3)) + 0.5 * zd[2]
        for c, v in enumerate((v0, v1, v2)):
            rr[c, z + 1] = v

    def rhs_inner(z, _):
        rhs_plane(z, lambda c: st_ref[c, z - 1], lambda c: st_ref[c, z + 1])
        return 0

    lax.fori_loop(1, last, rhs_inner, 0)
    stress_up.wait()
    stress_down.wait()
    rhs_plane(0, lambda c: sh[0, c], lambda c: st_ref[c, 1])
    rhs_plane(last, lambda c: st_ref[c, last - 1], lambda c: sh[1, c])
    r_up = remote(rr.at[:, depth], rr.at[:, 0], nsend.at[1, 0], nrecv.at[1, 0], "slab", up)
    r_down = remote(rr.at[:, 1], rr.at[:, depth + 1], nsend.at[1, 1], nrecv.at[1, 1], "slab", down)
    r_up.start()
    r_down.start()
    c8[0] = sh[0, 6] * 0.125
    c8[depth + 1] = sh[1, 6] * 0.125

    def diagonal(z, _):
        wide = spread(cut(c8[z - 1] + 2.0 * c8[z] + c8[z + 1]), sub)
        for i, w in enumerate(wide):
            at = slice(8 * i, 8 * i + 8)
            ee[z, at] = 8.0 * (8.0 + mass_weight) * c8[z, at] + w
        return 0

    lax.fori_loop(1, depth + 1, diagonal, 0)

    zero = jnp.zeros((8, LANES), jnp.float32)

    def apply_plane(z, carry):
        norm, curve = carry
        for c in range(3):
            plain, mixed = [], []
            for i in range(0, NVX, 8):
                at = slice(i, i + 8)
                ra, rb, rc = rr[c, z - 1, at], rr[c, z, at], rr[c, z + 1, at]
                crb = c8[z, at] * rb
                plain.append((ra + rc) + (rb + rb))
                mixed.append((c8[z - 1, at] * ra + c8[z + 1, at] * rc) + (crb + crb))
            plain = spread(plain, sub)
            mixed = spread(mixed, sub)
            for i in range(0, NVX, 8):
                at = slice(i, i + 8)
                rb = rr[c, z, at]
                image = ee[z, at] * rb - c8[z, at] * plain[i // 8] - mixed[i // 8]
                im[c, z, at] = image
                norm = norm + rb * rb
                curve = curve + rb * image
        return norm, curve

    def reduce_start(it, norm, curve, extra):
        row = lax.broadcasted_iota(jnp.int32, (8, LANES), 0)
        n = jnp.sum(norm, axis=0, keepdims=True)
        c = jnp.sum(curve, axis=0, keepdims=True)
        tile = jnp.where(row == 0, n, jnp.where(row == 1, c, 0.0))
        if extra is not None:
            tile = jnp.where(row == 2, extra, tile)
        ps[it] = tile
        copies = []
        for k in range(1, slabs):
            to = lax.rem(slab + k, slabs)
            copy = remote(ps.at[it], red.at[it, slab], rsend.at[it, k], rrecv.at[it, k], "slab", to)
            copy.start()
            copies.append(copy)
        red[it, slab] = tile
        return copies

    def reduce_end(it, copies):
        for copy in copies:
            copy.wait()
        total = red[it, 0]
        for k in range(1, slabs):
            total = total + red[it, k]
        kept = jnp.where(lane_id(8) < NVX, total, 0.0)
        sums = jnp.sum(kept, axis=1, keepdims=True)
        return total, sums[0:1], sums[1:2]

    carry = lax.fori_loop(2, depth, apply_plane, (zero, zero))
    r_up.wait()
    r_down.wait()
    carry = apply_plane(1, carry)
    carry = apply_plane(depth, carry)

    def send_image(it):
        first = remote(im.at[:, depth], hb.at[it, 0], nsend.at[2 + it, 0], nrecv.at[2 + it, 0], "slab", up)
        second = remote(im.at[:, 1], hb.at[it, 1], nsend.at[2 + it, 1], nrecv.at[2 + it, 1], "slab", down)
        first.start()
        second.start()
        return first, second

    halos = send_image(0)
    copies = reduce_start(0, *carry, sum_ref[...])
    total, norm_now, curve_now = reduce_end(0, copies)
    eo[...] = total
    element = []
    for k in range(1, groups):
        to = lax.rem(group + k, groups)
        copy = remote(eo, es.at[group], esend.at[k], erecv.at[k], "rve", to)
        copy.start()
        element.append(copy)
    es[group] = total
    alpha = norm_now / curve_now

    ratio = None
    for turn in range(ITERS - 1):
        for copy in halos:
            copy.wait()

        def refresh(c, z, fresh):
            if turn > 0:
                fresh = fresh + ratio * al[c, z]
            al[c, z] = fresh
            rr[c, z] = rr[c, z] - alpha * fresh

        for c in range(3):
            refresh(c, 0, hb[turn, 0, c])
            refresh(c, depth + 1, hb[turn, 1, c])

        def direction(z):
            rows = pl.ds(pl.multiple_of((z - 1) * NVX, NVX), NVX)
            for c in range(3):
                if turn == 0:
                    d = rr[c, z]
                    uu[c, rows, :] = alpha * d
                else:
                    d = rr[c, z] + ratio * dd[c, z - 1]
                    uu[c, rows, :] = uu[c, rows, :] + alpha * d
                dd[c, z - 1] = d

        def update(z, _):
            direction(z)
            for c in range(3):
                refresh(c, z, im[c, z])
            return 0

        lax.fori_loop(1, depth + 1, update, 0)
        carry = apply_plane(1, (zero, zero))
        carry = apply_plane(depth, carry)
        if turn + 1 < ITERS - 1:
            halos = send_image(turn + 1)
        carry = lax.fori_loop(2, depth, apply_plane, carry)
        copies = reduce_start(turn + 1, *carry, None)
        _, norm_next, product = reduce_end(turn + 1, copies)
        ratio = norm_next / norm_now
        alpha = norm_next / (product - ratio * norm_next / alpha)
        norm_now = norm_next

    def last_turn(z, _):
        rows = pl.ds(pl.multiple_of(z * NVX, NVX), NVX)
        for c in range(3):
            d = rr[c, z + 1] + ratio * dd[c, z]
            uu[c, rows, :] = uu[c, rows, :] + alpha * d
        return 0

    lax.fori_loop(0, depth, last_turn, 0)

    def to_flat(z, _):
        for c in range(3):
            for g8 in range(NVX // 32):
                rows4 = [
                    uu[c, pl.ds(z * NVX + 32 * g8 + r, 8, stride=4), :] for r in range(4)
                ]
                for t, v in enumerate(pack_rows(rows4)):
                    out_ref[c, z, pl.ds(24 * g8 + t, 8, stride=3)] = v
        return 0

    lax.fori_loop(0, depth, to_flat, 0)

    for move in moves:
        move.wait()
    for j in range(in_dev):
        source = pg_ref[group, slab * in_dev + j]
        got = ab[source]
        for c in range(7):
            inbox_ref[c, pl.ds(j, BLK // LANES, stride=in_dev), :] = got[c]
    for copy in element:
        copy.wait()
    mine = jnp.zeros((1, LANES), jnp.float32)
    for k in range(groups):
        mine = mine + jnp.where(own_ref[k] == group, es[k][2:3], 0.0)
    elem_ref[...] = mine[:, 0:42]


def on_device(
    groups, slabs,
    plastic_strain, hardening_var, strain_start, strain_step, shear_mod, bulk_mod, yield_stress,
    substeps, pull_group, pull_block, owner,
):
    depth = plastic_strain.shape[2]
    in_dev = pull_group.shape[1] // slabs
    volume = float(depth * slabs * PLANE)
    smem = pl.BlockSpec(memory_space=pltpu.SMEM)
    vmem = pl.BlockSpec(memory_space=pltpu.VMEM)
    f32 = jnp.float32
    tiles = PLANE // LANES
    planes = depth // 4 if depth % 4 == 0 else 1
    six = pl.BlockSpec((6, planes, tiles, LANES), lambda i: (0, i, 0, 0))
    one = pl.BlockSpec((planes, tiles, LANES), lambda i: (i, 0, 0))

    def whole(shape):
        return pl.BlockSpec(shape, lambda i: (0,) * len(shape))

    def stay(x):
        return pltpu.with_memory_space_constraint(x, pltpu.HBM)

    def view6(x):
        return stay(x.reshape(6, depth, tiles, LANES))

    def view1(x):
        return stay(x.reshape(depth, tiles, LANES))

    pick_shape = (groups, 7, BLK // LANES, LANES)
    shapes = ((7, depth, NVX, LANES), pick_shape, (1, LANES))
    stress, picked, partial_sums = pl.pallas_call(
        functools.partial(material_kernel, depth, volume, in_dev, planes),
        grid=(depth // planes,),
        in_specs=[smem, smem, smem, six, one, six, six, one, one, one],
        out_specs=[
            pl.BlockSpec((7, planes, NVX, LANES), lambda i: (0, i, 0, 0)),
            whole(shapes[1]),
            whole(shapes[2]),
        ],
        out_shape=[jax.ShapeDtypeStruct(s, f32) for s in shapes],
        scratch_shapes=[
            pltpu.VMEM((8 + len(PAIRS), 8, LANES), f32),
            pltpu.VMEM((7, planes, tiles, LANES), f32),
            pltpu.VMEM((tiles, LANES), jnp.int32),
            pltpu.VMEM((5, tiles, LANES), f32),
            pltpu.VMEM((5, tiles, LANES), f32),
            pltpu.VMEM((tiles, LANES), f32),
            pltpu.VMEM((tiles, LANES), f32),
            pltpu.VMEM((7, tiles, LANES), f32),
        ],
        compiler_params=pltpu.CompilerParams(
            dimension_semantics=("arbitrary",), vmem_limit_bytes=16 * 1024 * 1024
        ),
        name="material",
    )(
        substeps, pull_group, pull_block, view6(plastic_strain), view1(hardening_var),
        view6(strain_start), view6(strain_step), view1(shear_mod), view1(bulk_mod),
        view1(yield_stress),
    )
    plane = (NVX, LANES)
    dma = pltpu.SemaphoreType.DMA
    correction, inbox, element_sums = pl.pallas_call(
        functools.partial(solve_kernel, depth, groups, slabs, in_dev),
        in_specs=[smem, smem, vmem, vmem, vmem],
        out_specs=[vmem, vmem, vmem],
        out_shape=[
            jax.ShapeDtypeStruct((3, depth, tiles, LANES), f32),
            jax.ShapeDtypeStruct((7, in_dev * BLK // LANES, LANES), f32),
            jax.ShapeDtypeStruct((1, 42), f32),
        ],
        scratch_shapes=[
            pltpu.VMEM((2, 7) + plane, f32),
            pltpu.VMEM((depth + 2,) + plane, f32),
            pltpu.VMEM((depth + 2,) + plane, f32),
            pltpu.VMEM((3, depth + 2) + plane, f32),
            pltpu.VMEM((3, depth + 2) + plane, f32),
            pltpu.VMEM((3, depth + 2) + plane, f32),
            pltpu.VMEM((3, depth) + plane, f32),
            pltpu.VMEM((3, depth * NVX, LANES), f32),
            pltpu.VMEM((ITERS - 1, 2, 3) + plane, f32),
            pltpu.VMEM((ITERS, 8, LANES), f32),
            pltpu.VMEM((ITERS, slabs, 8, LANES), f32),
            pltpu.VMEM(pick_shape, f32),
            pltpu.VMEM((groups, 8, LANES), f32),
            pltpu.VMEM((8, LANES), f32),
            dma((ITERS + 1, 2)),
            dma((ITERS + 1, 2)),
            dma((ITERS, slabs)),
            dma((ITERS, slabs)),
            dma((groups,)),
            dma((groups,)),
            dma((groups,)),
            dma((groups,)),
        ],
        compiler_params=pltpu.CompilerParams(
            collective_id=0, has_side_effects=True, vmem_limit_bytes=26 * 1024 * 1024
        ),
        name="solve",
    )(pull_group, owner, stress, picked, partial_sums)
    correction = correction.reshape(3, 1, depth, PLANE)
    inbox = inbox.reshape(7, BLK // LANES, in_dev, LANES).swapaxes(1, 2)
    return correction, inbox.reshape(7, 1, in_dev, BLK), element_sums


def solution(mesh):
    return jax.shard_map(
        functools.partial(on_device, mesh.shape["rve"], mesh.shape["slab"]),
        mesh=mesh,
        in_specs=(
            P(None, "rve", "slab", None),
            P("rve", "slab", None),
            P(None, "rve", "slab", None),
            P(None, "rve", "slab", None),
            P("rve", "slab", None),
            P("rve", "slab", None),
            P("rve", "slab", None),
            P(),
            P(),
            P(),
            P(),
        ),
        out_specs=(P(None, "rve", "slab", None), P(None, "rve", "slab", None), P("rve", None)),
        check_vma=False,
    )
```
